32 devices in a mesh: section: 8 (over y, x, core), dp: 4 (over z).
Axes of the slice: x: 2, y: 2, z: 4, core: 2. Of those that a mesh axis runs over, the one named last changes fastest.
Arguments:
- activations: bfloat16 [2048, 8192], P('dp'), may hold values from -6 to 6
- cotangent: bfloat16 [2048, 8192], P('dp'), may hold values from -6 to 6
- gate_pre: bfloat16 [2048, 4096], P('dp', 'section'), may hold values from -6 to 6
- weights: bfloat16 [2, 8192, 4096], P(None, 'dp', 'section'), may hold values from -0.0625 to 0.0625
- holder_map: int32 [64, 8, 2], P('dp', 'section'), may hold values from 0 to 7, as said below
- master: float32 [8, 4, 48, 128, 512], P('section', 'dp'), may hold values from -0.0625 to 0.0625
- moment_one: float32 [8, 4, 48, 128, 512], P('section', 'dp'), may hold values from -80 to 80
- moment_two: float32 [8, 4, 48, 128, 512], P('section', 'dp'), may hold values from 102.4 to 4096
- adam_step: int32 [1], replicated, may hold values from 1 to 11
Outputs:
- passed_back: bfloat16 [2048, 8192], P('dp', 'section')
- new_weights: bfloat16 [2, 8192, 4096], P(None, 'dp', 'section')
The draws below stay inside these ranges and needn't reach their ends.
Inputs may be any that keep to these rules, and one draw needn't show every extreme that they name: `holder_map`: every block of one device (32 of them) goes to holders of that device's dp index; one device sends to exactly 4 holder sections, exactly 8 blocks to each; each holder device receives at most 48 blocks from all sections, and in every dp column some holder receives exactly 48.
All inputs are finite; a program needn't handle non-finite values.
Results may differ from the reference program's by a relative error of at most 0.012.
Values may be sent and summed in bfloat16 or wider, within the bound.
A program may use at most 320 MiB of HBM per device.

```python
import math
import jax
import jax.numpy as jnp
from jax import lax

D = 8192
HID = 4096
TOK_DEV = 512
BLOCK = 128
SECTIONS = 8
DP_RANKS = 4
HID_SHARD = 512
TOKENS = 2048
ROW_BLOCKS = 16
SEND_MOST = 8
CAP = 48


def draw_holder_map(key, part):
    per_source = 2 * ROW_BLOCKS
    light_count = SECTIONS // 2
    order_key, block_key = jax.random.split(key)
    column_keys = jax.random.split(order_key, DP_RANKS)
    ranking = jax.vmap(lambda subkey: jax.random.permutation(subkey, SECTIONS))(column_keys)
    lighter = ranking[:, :light_count]
    heavier = ranking[:, light_count:]
    window = jnp.arange(SECTIONS) % light_count
    offsets = jnp.arange(1, light_count)
    light_entries = lighter[:, (window[:, None] + offsets[None, :]) % light_count]
    heavy_entry = heavier[:, window][:, :, None]
    entries = jnp.concatenate([light_entries, heavy_entry], axis=2)
    source_keys = jax.random.split(block_key, DP_RANKS * SECTIONS)
    shuffles = jax.vmap(lambda subkey: jax.random.permutation(subkey, per_source))(source_keys)
    group_of = shuffles.reshape(DP_RANKS, SECTIONS, per_source) // SEND_MOST
    holder = jnp.take_along_axis(entries, group_of, axis=2)
    holder = holder.reshape(DP_RANKS, SECTIONS, ROW_BLOCKS, 2).transpose(0, 2, 1, 3)
    return holder.reshape(DP_RANKS * ROW_BLOCKS, SECTIONS, 2).astype(jnp.int32)


def strengthened(drawn, own_key, source, target, shards_of, factor):
    def block_of(axis_at):
        return (jnp.arange(drawn.shape[axis_at]) // (drawn.shape[axis_at] // shards_of)).reshape((-1,) + (1,) * (drawn.ndim - 1 - axis_at))

    first = jax.random.permutation(own_key, shards_of)[block_of(target)]
    second = (block_of(target) + shards_of // 2) % shards_of
    return jnp.where((block_of(source) == first) | (block_of(source) == second), factor * drawn, drawn)


def shard_levels(rng, dims, pieces, low, top_value):
    def one(position, parts):
        heights = jax.random.uniform(jax.random.fold_in(jax.random.fold_in(rng, 6), position), (parts,), jnp.float32, low / len(pieces), top_value / len(pieces))
        return jnp.repeat(jnp.exp(heights), dims[position] // parts).reshape((-1,) + (1,) * (len(dims) - position - 1))

    loudness = one(*pieces[0])
    for cut in pieces[1:]:
        loudness = loudness * one(*cut)
    return loudness


def scatter_about(key, shape, spread, bound, cuts=(), held_as=jnp.bfloat16):
    loudness = shard_levels(key, shape, cuts, -0.22, 0.18) if cuts else 1.0
    drawn = jax.random.normal(key, shape, jnp.float32) * spread * loudness
    return jnp.minimum(jnp.maximum(drawn, -bound), bound).astype(held_as)


def bell_draw_with(own_key, extent, scale, reach, pieces, heavy, held_as=jnp.bfloat16):
    array = scale * jax.random.normal(own_key, extent, jnp.float32)
    if pieces:
        array = array * shard_levels(own_key, extent, pieces, -0.22, 0.18)
    return jnp.clip(strengthened(array, jax.random.fold_in(own_key, 3), *heavy), -reach, reach).astype(held_as)


def setup_inputs(seed: int = 0) -> dict:
    key_list = jax.random.split(jax.random.key(seed), 10)
    return {
        "activations": bell_draw_with(key_list[0], (TOKENS, D), 1.0, 6.0, ((0, 4),), (0, 1, 4, 2.0)),
        "cotangent": scatter_about(key_list[1], (TOKENS, D), 1.0, 6.0, ((0, 4),)),
        "gate_pre": scatter_about(key_list[2], (TOKENS, HID), 1.5, 6.0, ((0, 4), (1, 8))),
        "weights": scatter_about(key_list[3], (2, D, HID), D ** -0.5, 0.0625, ((1, 4), (2, 8))),
        "holder_map": draw_holder_map(jax.random.fold_in(key_list[9], 71), 0),
        "master": scatter_about(key_list[5], (SECTIONS, DP_RANKS, CAP, BLOCK, HID_SHARD), D ** -0.5, 0.0625, ((0, 8), (1, 4)), jnp.float32),
        "moment_one": scatter_about(key_list[6], (SECTIONS, DP_RANKS, CAP, BLOCK, HID_SHARD), (TOKENS ** 0.5 * 0.3), 80.0, ((0, 8), (1, 4)), jnp.float32),
        "moment_two": jnp.clip(jnp.exp(math.log(4096.0) - 3.6888794 * jax.random.uniform(key_list[7], (SECTIONS, DP_RANKS, CAP, BLOCK, HID_SHARD), jnp.float32) ** shard_levels(key_list[7], (SECTIONS, DP_RANKS, CAP, BLOCK, HID_SHARD), ((0, 8), (1, 4)), -0.2, 0.2)), 102.4, 4096.0),
        "adam_step": jax.random.randint(key_list[8], (1,), 1, 12).astype(jnp.int32),
    }


learn_rate = 0.03
beta_one = 0.9
beta_two = 0.95
adam_eps = 1e-08
decay_rate = 0.1

def adam_apply(gradient, weight_master, first_moment, second_moment, step_number):
    step_float = step_number.astype(jnp.float32)
    fix_one = 1.0 - jnp.power(jnp.float32(beta_one), step_float)
    fix_two = 1.0 - jnp.power(jnp.float32(beta_two), step_float)
    first_new = beta_one * first_moment + (1.0 - beta_one) * gradient
    second_new = beta_two * second_moment + (1.0 - beta_two) * gradient * gradient
    update = first_new / fix_one / (jnp.sqrt(second_new / fix_two) + adam_eps)
    return (weight_master * (1.0 - learn_rate * decay_rate) - learn_rate * update).astype(jnp.bfloat16)

def reference(activations, cotangent, gate_pre, weights, holder_map, master, moment_one, moment_two, adam_step):
    up_full = weights[0]
    down_full = weights[1]
    lifted = jnp.dot(activations, up_full, preferred_element_type=jnp.float32)
    back_hidden = jnp.dot(cotangent, down_full, preferred_element_type=jnp.float32)
    gate_silu = jax.nn.silu(gate_pre.astype(jnp.float32))
    hidden = (gate_silu * lifted).astype(jnp.bfloat16)
    back_up = (back_hidden * gate_silu).astype(jnp.bfloat16)
    up_groups = up_full.reshape(D, SECTIONS, HID_SHARD).transpose(1, 0, 2)
    back_groups = back_up.reshape(TOKENS, SECTIONS, HID_SHARD).transpose(1, 0, 2)

    def add_section(running, pair):
        part_up, part_back = pair
        term = lax.dot_general(part_back, part_up, (((1,), (1,)), ((), ())), preferred_element_type=jnp.float32)
        rounded = lax.optimization_barrier(term.astype(jnp.bfloat16))
        return (running + rounded.astype(jnp.float32), None)
    total_in, unused_in = lax.scan(add_section, jnp.zeros((TOKENS, D), jnp.float32), (up_groups, back_groups))
    passed_back = total_in.astype(jnp.bfloat16)

    def add_group(running, group):
        group_in, group_out, group_up, group_hidden = group
        term = jnp.stack([lax.dot_general(group_in, group_up, (((0,), (0,)), ((), ())), preferred_element_type=jnp.float32), lax.dot_general(group_out, group_hidden, (((0,), (0,)), ((), ())), preferred_element_type=jnp.float32)], axis=0)
        rounded = lax.optimization_barrier(term.astype(jnp.bfloat16))
        return (running + rounded.astype(jnp.float32), None)
    groups = (activations.reshape(DP_RANKS, TOK_DEV, D), cotangent.reshape(DP_RANKS, TOK_DEV, D), back_up.reshape(DP_RANKS, TOK_DEV, HID), hidden.reshape(DP_RANKS, TOK_DEV, HID))
    summed, unused = lax.scan(add_group, jnp.zeros((2, D, HID), jnp.float32), groups)
    total_blocks = D // BLOCK
    per_source = 2 * ROW_BLOCKS
    by_column = holder_map.reshape(DP_RANKS, ROW_BLOCKS, SECTIONS, 2).transpose(0, 2, 1, 3).reshape(DP_RANKS, SECTIONS * per_source)
    one_hot = (by_column[:, :, None] == jnp.arange(SECTIONS, dtype=jnp.int32)[None, None, :]).astype(jnp.int32)
    ahead = jnp.cumsum(one_hot, axis=1) - one_hot
    order_in = lax.optimization_barrier(jnp.sum(ahead * one_hot, axis=2)).astype(jnp.int32)
    slot_of = order_in.reshape(DP_RANKS, SECTIONS, ROW_BLOCKS, 2).transpose(0, 2, 1, 3).reshape(total_blocks, SECTIONS, 2)
    column_of = (jnp.arange(total_blocks, dtype=jnp.int32) // ROW_BLOCKS).astype(jnp.int32)[:, None, None]
    column_of = jnp.broadcast_to(column_of, holder_map.shape)
    grad_blocks = summed.reshape(2, total_blocks, BLOCK, SECTIONS, HID_SHARD).transpose(1, 3, 0, 2, 4)
    weight_master = master[holder_map, column_of, slot_of]
    first_moment = moment_one[holder_map, column_of, slot_of]
    second_moment = moment_two[holder_map, column_of, slot_of]
    updated = adam_apply(grad_blocks, weight_master, first_moment, second_moment, adam_step[0])
    new_weights = updated.transpose(2, 0, 3, 1, 4).reshape(2, D, HID)
    return (passed_back, new_weights)
```

```python
import jax
import jax.numpy as jnp
from jax import lax
from jax.experimental import pallas as pl
from jax.experimental.pallas import tpu as pltpu
from jax.sharding import PartitionSpec as P

learn_rate = 0.03
beta_one = 0.9
beta_two = 0.95
adam_eps = 1e-08
decay_rate = 0.1

BF16 = jnp.bfloat16
F32 = jnp.float32


def adam_kernel(item_ref, count_ref, fix_ref, grad_ref, w_ref, a_ref, b_ref, out_ref):
    @pl.when(pl.program_id(0) < count_ref[0])
    def _():
        grad = grad_ref[0].astype(F32)
        first = beta_one * a_ref[0] + (1.0 - beta_one) * grad
        second = beta_two * b_ref[0] + (1.0 - beta_two) * grad * grad
        update = first / fix_ref[0] / (jnp.sqrt(second / fix_ref[1]) + adam_eps)
        out_ref[0] = (
            w_ref[0] * (1.0 - learn_rate * decay_rate) - learn_rate * update
        ).astype(BF16)


def adam_slots(items, count, fixes, arrivals, states, chunk):
    total, rows, cols = arrivals.shape
    capacity = states[0].shape[0]

    def at_slot(c, item_ref, count_ref):
        return (jnp.minimum(c, jnp.maximum(count_ref[0] - 1, 0)), 0, chunk)

    def at_item(c, item_ref, count_ref):
        return (item_ref[c], 0, 0)

    state_spec = pl.BlockSpec((1, rows, cols), at_slot)
    item_spec = pl.BlockSpec((1, rows, cols), at_item)
    return pl.pallas_call(
        adam_kernel,
        out_shape=jax.ShapeDtypeStruct(arrivals.shape, BF16),
        grid_spec=pltpu.PrefetchScalarGridSpec(
            num_scalar_prefetch=2,
            grid=(capacity,),
            in_specs=[pl.BlockSpec(memory_space=pltpu.SMEM), item_spec] + [state_spec] * 3,
            out_specs=item_spec,
        ),
        cost_estimate=pl.CostEstimate(
            flops=20 * capacity * rows * cols,
            bytes_accessed=16 * capacity * rows * cols,
            transcendentals=capacity * rows * cols,
        ),
        name="adam",
    )(items, count, fixes, arrivals, *states)


def move_kernel(index_ref, in_ref, out_ref):
    out_ref[...] = in_ref[...].reshape(out_ref.shape)


def pick_rows(index, table, rows, matrices_first):
    count = index.shape[0]
    cols = table.shape[2]
    return pl.pallas_call(
        move_kernel,
        out_shape=jax.ShapeDtypeStruct((count, rows, cols), table.dtype),
        grid_spec=pltpu.PrefetchScalarGridSpec(
            num_scalar_prefetch=1,
            grid=(count,),
            in_specs=[pl.BlockSpec((1, rows, cols), lambda i, ix: (ix[i] % 2, ix[i] // 2, 0))],
            out_specs=pl.BlockSpec((1, rows, cols), lambda i, ix: (i, 0, 0)),
        ),
        name="pick_rows",
    )(index, table)


def place_rows(index, parts, row_blocks):
    rows, cols = parts[0].shape[1:]
    width = cols * len(parts)

    def body(index_ref, *refs):
        out_ref = refs[-1]
        for at, ref in enumerate(refs[:-1]):
            out_ref[0, :, at * cols : (at + 1) * cols] = ref[0]

    return pl.pallas_call(
        body,
        out_shape=jax.ShapeDtypeStruct((2, row_blocks * rows, width), parts[0].dtype),
        grid_spec=pltpu.PrefetchScalarGridSpec(
            num_scalar_prefetch=1,
            grid=(row_blocks * 2,),
            in_specs=[pl.BlockSpec((1, rows, cols), lambda i, ix: (ix[i], 0, 0))] * len(parts),
            out_specs=pl.BlockSpec((1, rows, width), lambda i, ix: (i % 2, i // 2, 0)),
        ),
        name="place_rows",
    )(index, *parts)


def per_device(
    activations, cotangent, gate_pre, weights, holder_map, master, moment_one, moment_two, adam_step
):
    sections = lax.axis_size("section")
    ranks = lax.axis_size("dp")
    here = lax.axis_index("section")
    tok_dev, width = activations.shape
    piece = tok_dev // sections
    row_count, hidden_units = weights.shape[1:]
    block_rows = master.shape[3]
    capacity = master.shape[2]
    row_blocks = row_count // block_rows
    per_dest = 4 * row_blocks // sections
    over_tokens = (((0,), (0,)), ((), ()))

    owners = holder_map[:, 0, :].reshape(-1)
    section_ids = jnp.arange(sections, dtype=jnp.int32)
    choose = (owners[:, None] == section_ids[None, :]).astype(jnp.int32)
    order_in = jnp.sum((jnp.cumsum(choose, axis=0) - choose) * choose, axis=1)
    totals = jnp.sum(choose, axis=0)
    every_total = lax.all_gather(totals, "section")
    place = owners * per_dest + order_in
    wanted = jnp.arange(sections * per_dest, dtype=jnp.int32)
    source = jnp.sum(
        jnp.where(
            place[None, :] == wanted[:, None],
            jnp.arange(place.shape[0], dtype=jnp.int32)[None, :],
            0,
        ),
        axis=1,
    )
    mine = jnp.sum(jnp.where(section_ids[None, :] == here, every_total, 0), axis=1)
    before = jnp.cumsum(mine) - mine
    count = jnp.sum(mine)
    spot = jnp.arange(per_dest, dtype=jnp.int32)
    slot = jnp.where(spot[None, :] < mine[:, None], before[:, None] + spot[None, :], -1).reshape(-1)
    slots = jnp.minimum(jnp.arange(capacity, dtype=jnp.int32), jnp.maximum(count - 1, 0))
    items = jnp.sum(jnp.where(slot[None, :] == slots[:, None], wanted[None, :], 0), axis=1)
    step_float = adam_step[0].astype(F32)
    fixes = jnp.stack(
        [
            1.0 - jnp.power(jnp.float32(beta_one), step_float),
            1.0 - jnp.power(jnp.float32(beta_two), step_float),
        ]
    )

    def spread(tokens):
        own = lax.dynamic_slice_in_dim(tokens, here * piece, piece, 0)
        swapped = lax.all_to_all(own, "dp", split_axis=1, concat_axis=0, tiled=True)
        return lax.all_gather(swapped, "section", axis=0, tiled=True)

    def project(full, matrix):
        part = jnp.dot(full, matrix, preferred_element_type=F32).astype(BF16)
        part = part.reshape(sections, ranks, piece, hidden_units).transpose(1, 0, 2, 3)
        part = part.reshape(ranks * tok_dev, hidden_units)
        return lax.psum_scatter(part, "dp", scatter_dimension=0, tiled=True).astype(F32)

    def all_tokens(local):
        out = lax.all_gather(local, "dp", axis=0, tiled=True)
        out = out.reshape(ranks, sections, piece, hidden_units).transpose(1, 0, 2, 3)
        return out.reshape(ranks * tok_dev, hidden_units)

    cot_full = spread(cotangent)
    act_full = spread(activations)
    back_hidden = project(cot_full, weights[1])
    lifted = project(act_full, weights[0])
    gate_silu = jax.nn.silu(gate_pre.astype(F32))
    back_up = all_tokens((back_hidden * gate_silu).astype(BF16))
    hidden = all_tokens((gate_silu * lifted).astype(BF16))

    split = sections // ranks
    in_part = lax.dot_general(
        back_up, weights[0], (((1,), (1,)), ((), ())), preferred_element_type=F32
    ).astype(BF16)
    in_part = in_part.reshape(sections, ranks, piece, split, row_count // split)
    in_part = in_part.transpose(1, 3, 0, 2, 4).reshape(sections, tok_dev, row_count // split)
    reduced = lax.psum_scatter(in_part, "section", scatter_dimension=0, tiled=True)
    routes = [
        (s * ranks + k, (split * k + s % split) * ranks + s // split)
        for s in range(sections)
        for k in range(ranks)
    ]
    passed_back = lax.ppermute(reduced, ("section", "dp"), routes)[0]

    grads = jnp.stack(
        [
            lax.dot_general(act_full, back_up, over_tokens, preferred_element_type=F32).astype(BF16),
            lax.dot_general(cot_full, hidden, over_tokens, preferred_element_type=F32).astype(BF16),
        ]
    )
    outgoing = pick_rows(source, grads, block_rows, True)
    arrivals = lax.all_to_all(outgoing, "section", split_axis=0, concat_axis=0, tiled=True)
    updated = adam_slots(
        items,
        count.reshape(1),
        fixes,
        arrivals,
        (master[0, 0], moment_one[0, 0], moment_two[0, 0]),
        0,
    )
    returned = lax.all_to_all(updated, "section", split_axis=0, concat_axis=0, tiled=True)
    new_rows = place_rows(place, [returned], row_blocks)
    return (passed_back, new_rows)


def solution(mesh):
    in_specs = (
        P("dp", None),
        P("dp", None),
        P("dp", "section"),
        P(None, "dp", "section"),
        P("dp", "section", None),
        P("section", "dp", None, None, None),
        P("section", "dp", None, None, None),
        P("section", "dp", None, None, None),
        P(),
    )
    out_specs = (P("dp", "section"), P(None, "dp", "section"))
    return jax.shard_map(
        per_device, mesh=mesh, in_specs=in_specs, out_specs=out_specs, check_vma=False
    )
```

```python
import jax
import jax.numpy as jnp
from jax import lax
from jax.experimental import pallas as pl
from jax.experimental.pallas import tpu as pltpu
from jax.sharding import PartitionSpec as P

learn_rate = 0.03
beta_one = 0.9
beta_two = 0.95
adam_eps = 1e-08
decay_rate = 0.1

BF16 = jnp.bfloat16
F32 = jnp.float32


CHUNKS = 2
MESH = pl.DeviceIdType.MESH


def spread_kernel(shape, cot_ref, act_ref, cot_out, act_out, local_sem, send_sem, recv_sem):
    sections, ranks, tok_dev, cols = shape
    chips = sections // 2
    piece = tok_dev // sections
    s = lax.axis_index("section")
    k = lax.axis_index("dp")
    core = lax.rem(s, 2)
    chip = s // 2
    sibling = (s + 1 - 2 * core, k)
    along = {d: (s, lax.rem(k + d, ranks)) for d in range(1, ranks)}
    across = {j: (2 * lax.rem(chip + j, chips) + core, k) for j in range(1, chips)}

    barrier = pltpu.get_barrier_semaphore()
    greeted = list(along.values()) + list(across.values()) + [sibling]
    for peer in greeted:
        pl.semaphore_signal(barrier, inc=1, device_id=peer, device_id_type=MESH)
    pl.semaphore_wait(barrier, len(greeted))

    pairs = ((cot_ref, cot_out), (act_ref, act_out))
    sems = iter(range(send_sem.shape[0]))

    def send(src, dst, peer):
        at = next(sems)
        copy = pltpu.make_async_remote_copy(
            src_ref=src,
            dst_ref=dst,
            send_sem=send_sem.at[at],
            recv_sem=recv_sem.at[at],
            device_id=peer,
            device_id_type=MESH,
        )
        copy.start()
        return copy

    def rows(out, rank, section):
        start = pl.multiple_of(rank * tok_dev + section * piece, piece)
        return out.at[pl.ds(start, piece), :]

    hops = {}
    for d in range(1, ranks):
        for a, (ref, out) in enumerate(pairs):
            start = pl.multiple_of(along[d][1] * cols, cols)
            from_rows = pl.ds(pl.multiple_of(s * piece, piece), piece)
            hops[a, d] = send(ref.at[from_rows, pl.ds(start, cols)], rows(out, k, s), along[d])
    local = []
    for a, (ref, out) in enumerate(pairs):
        copy = pltpu.make_async_copy(
            ref.at[:, pl.ds(pl.multiple_of(k * cols, cols), cols)],
            out.at[pl.ds(pl.multiple_of(k * tok_dev, tok_dev), tok_dev), :],
            local_sem.at[a],
        )
        copy.start()
        local.append(copy)
    wide, last = {}, []
    for d in range(1, ranks):
        origin = lax.rem(k + ranks - d, ranks)
        for a, (ref, out) in enumerate(pairs):
            hops[a, d].wait_recv()
            block = rows(out, origin, s)
            for j in range(1, chips):
                wide[a, d, j] = send(block, block, across[j])
            last.append(send(block, block, sibling))
    for d in range(1, ranks):
        origin = lax.rem(k + ranks - d, ranks)
        for a, (ref, out) in enumerate(pairs):
            for j in range(1, chips):
                wide[a, d, j].wait_recv()
                block = rows(out, origin, 2 * lax.rem(chip + chips - j, chips) + core)
                last.append(send(block, block, sibling))
    for copy in last:
        copy.wait_recv()
    for copy in list(hops.values()) + list(wide.values()) + last:
        copy.wait_send()
    for copy in local:
        copy.wait()


def spread(cotangent, activations, sections, ranks):
    tok_dev, width = activations.shape
    cols = width // ranks
    copies = 2 * (ranks - 1) * sections
    out = jax.ShapeDtypeStruct((ranks * tok_dev, cols), activations.dtype)
    anywhere = pl.BlockSpec(memory_space=pl.ANY)
    moved = 2 * ranks * tok_dev * cols * 2

    def body(*refs):
        spread_kernel((sections, ranks, tok_dev, cols), *refs)

    return pl.pallas_call(
        body,
        out_shape=(out, out),
        in_specs=[anywhere, anywhere],
        out_specs=(anywhere, anywhere),
        scratch_shapes=[
            pltpu.SemaphoreType.DMA((2,)),
            pltpu.SemaphoreType.DMA((copies,)),
            pltpu.SemaphoreType.DMA((copies,)),
        ],
        compiler_params=pltpu.CompilerParams(collective_id=1, has_side_effects=True),
        cost_estimate=pl.CostEstimate(flops=0, bytes_accessed=8 * moved, transcendentals=0),
        name="spread",
    )(cotangent, activations)


def adam_kernel(source_ref, count_ref, fix_ref, grad_ref, w_ref, a_ref, b_ref, out_ref):
    @pl.when(pl.program_id(0) < count_ref[0])
    def _():
        scale_one = learn_rate / fix_ref[0]
        scale_two = 1.0 / fix_ref[1]

        def one(i, carry):
            grad = grad_ref[i].astype(F32)
            first = beta_one * a_ref[i] + (1.0 - beta_one) * grad
            second = beta_two * b_ref[i] + (1.0 - beta_two) * grad * grad
            update = (first * scale_one) / (jnp.sqrt(second * scale_two) + adam_eps)
            out_ref[i] = (w_ref[i] * (1.0 - learn_rate * decay_rate) - update).astype(BF16)
            return carry

        lax.fori_loop(0, grad_ref.shape[0], one, 0)


def adam_slots(sources, count, fixes, arrivals, states, chunk, per_dest):
    total, rows, cols = arrivals.shape
    capacity = states[0].shape[0]
    groups = capacity // per_dest
    cuts = 2

    def at_slot(g, h, source_ref, count_ref):
        live = g < count_ref[0]
        return (
            jnp.minimum(g, jnp.maximum(count_ref[0] - 1, 0)),
            jnp.where(live, h, cuts - 1),
            chunk,
        )

    def at_item(g, h, source_ref, count_ref):
        return (source_ref[g], jnp.where(g < count_ref[0], h, cuts - 1), 0)

    state_spec = pl.BlockSpec((per_dest, rows // cuts, cols), at_slot)
    item_spec = pl.BlockSpec((per_dest, rows // cuts, cols), at_item)
    return pl.pallas_call(
        adam_kernel,
        out_shape=jax.ShapeDtypeStruct(arrivals.shape, BF16),
        grid_spec=pltpu.PrefetchScalarGridSpec(
            num_scalar_prefetch=2,
            grid=(groups, cuts),
            in_specs=[pl.BlockSpec(memory_space=pltpu.SMEM), item_spec] + [state_spec] * 3,
            out_specs=item_spec,
        ),
        cost_estimate=pl.CostEstimate(
            flops=20 * capacity * rows * cols,
            bytes_accessed=16 * capacity * rows * cols,
            transcendentals=capacity * rows * cols,
        ),
        name="adam",
    )(sources, count, fixes, arrivals, *states)


def pick_rows(place, grads, rows, slots):
    cols = grads[0].shape[1]
    count = place.shape[0]
    anywhere = pl.BlockSpec(memory_space=pl.ANY)

    def body(place_ref, up_ref, down_ref, out_ref, sems):
        copies = []
        for i in range(count):
            ref = (up_ref, down_ref)[i % 2]
            copy = pltpu.make_async_copy(
                ref.at[pl.ds(i // 2 * rows, rows), :], out_ref.at[place_ref[i]], sems.at[i]
            )
            copy.start()
            copies.append(copy)
        for copy in copies:
            copy.wait()

    return pl.pallas_call(
        body,
        out_shape=jax.ShapeDtypeStruct((slots, rows, cols), grads[0].dtype),
        in_specs=[pl.BlockSpec(memory_space=pltpu.SMEM), anywhere, anywhere],
        out_specs=anywhere,
        scratch_shapes=[pltpu.SemaphoreType.DMA((count,))],
        cost_estimate=pl.CostEstimate(
            flops=0, bytes_accessed=4 * count * rows * cols, transcendentals=0
        ),
        name="pick_rows",
    )(place, *grads)


def place_rows(place, parts, row_blocks):
    rows, cols = parts[0].shape[1:]
    width = cols * len(parts)
    count = row_blocks * 2
    anywhere = pl.BlockSpec(memory_space=pl.ANY)

    def body(place_ref, *refs):
        out_ref, sems = refs[-2:]
        copies = []
        for at, ref in enumerate(refs[:-2]):
            for i in range(count):
                copy = pltpu.make_async_copy(
                    ref.at[place_ref[i]],
                    out_ref.at[i % 2, pl.ds(i // 2 * rows, rows), pl.ds(at * cols, cols)],
                    sems.at[at * count + i],
                )
                copy.start()
                copies.append(copy)
        for copy in copies:
            copy.wait()

    return pl.pallas_call(
        body,
        out_shape=jax.ShapeDtypeStruct((2, row_blocks * rows, width), parts[0].dtype),
        in_specs=[pl.BlockSpec(memory_space=pltpu.SMEM)] + [anywhere] * len(parts),
        out_specs=anywhere,
        scratch_shapes=[pltpu.SemaphoreType.DMA((count * len(parts),))],
        cost_estimate=pl.CostEstimate(
            flops=0, bytes_accessed=4 * count * rows * width, transcendentals=0
        ),
        name="place_rows",
    )(place, *parts)


def per_device(
    activations, cotangent, gate_pre, weights, holder_map, master, moment_one, moment_two, adam_step
):
    sections = lax.axis_size("section")
    ranks = lax.axis_size("dp")
    here = lax.axis_index("section")
    tok_dev, width = activations.shape
    row_count, hidden_units = weights.shape[1:]
    block_rows = master.shape[3]
    capacity = master.shape[2]
    row_blocks = row_count // block_rows
    per_dest = 4 * row_blocks // sections
    over_tokens = (((0,), (0,)), ((), ()))
    span = hidden_units // CHUNKS if hidden_units % (128 * CHUNKS) == 0 else hidden_units
    chunks = hidden_units // span

    owners = holder_map[:, 0, :].reshape(-1)
    section_ids = jnp.arange(sections, dtype=jnp.int32)
    choose = (owners[:, None] == section_ids[None, :]).astype(jnp.int32)
    totals = jnp.sum(choose, axis=0)
    every_total = lax.all_gather(totals, "section")
    every_total, activations, cotangent = lax.optimization_barrier(
        (every_total, activations, cotangent)
    )
    order_in = jnp.sum((jnp.cumsum(choose, axis=0) - choose) * choose, axis=1)
    place = owners * per_dest + order_in
    mine = jnp.sum(jnp.where(section_ids[None, :] == here, every_total, 0), axis=1)
    live = (mine > 0).astype(jnp.int32)
    rank_of = jnp.cumsum(live) - live
    count = jnp.sum(live)
    groups = jnp.minimum(
        jnp.arange(capacity // per_dest, dtype=jnp.int32), jnp.maximum(count - 1, 0)
    )
    sources = jnp.sum(
        jnp.where(
            (rank_of[None, :] == groups[:, None]) & (live[None, :] > 0), section_ids[None, :], 0
        ),
        axis=1,
    )
    step_float = adam_step[0].astype(F32)
    fixes = jnp.stack(
        [
            1.0 - jnp.power(jnp.float32(beta_one), step_float),
            1.0 - jnp.power(jnp.float32(beta_two), step_float),
        ]
    )
    states = (master[0, 0], moment_one[0, 0], moment_two[0, 0])
    gate_silu = jax.nn.silu(gate_pre.astype(F32))

    cot_full, act_full = spread(cotangent, activations, sections, ranks)

    gathered = []
    for j in range(chunks):
        at = slice(j * span, (j + 1) * span)
        part = jnp.concatenate(
            [
                jnp.dot(cot_full, weights[1][:, at], preferred_element_type=F32).astype(BF16),
                jnp.dot(act_full, weights[0][:, at], preferred_element_type=F32).astype(BF16),
            ],
            axis=1,
        )
        both = lax.psum_scatter(part, "dp", scatter_dimension=0, tiled=True).astype(F32)
        gate = gate_silu[:, at]
        local = (both * jnp.concatenate([gate, gate], axis=1)).astype(BF16)
        gathered.append(lax.all_gather(local, "dp", axis=0, tiled=True))

    returned = []
    for j in range(chunks):
        grads = (
            lax.dot_general(
                act_full, gathered[j][:, :span], over_tokens, preferred_element_type=F32
            ).astype(BF16),
            lax.dot_general(
                cot_full, gathered[j][:, span:], over_tokens, preferred_element_type=F32
            ).astype(BF16),
        )
        outgoing = pick_rows(place, grads, block_rows, sections * per_dest)
        arrivals = lax.all_to_all(outgoing, "section", split_axis=0, concat_axis=0, tiled=True)
        updated = adam_slots(sources, count.reshape(1), fixes, arrivals, states, j, per_dest)
        returned.append(
            lax.all_to_all(updated, "section", split_axis=0, concat_axis=0, tiled=True)
        )

    split = sections // ranks
    back_up = jnp.concatenate([each[:, :span] for each in gathered], axis=1)
    back_up = back_up.reshape(ranks, tok_dev, hidden_units)
    up_rows = weights[0].reshape(split, row_count // split, hidden_units)
    in_part = jnp.stack(
        [
            lax.dot_general(
                back_up[i // split],
                up_rows[i % split],
                (((1,), (1,)), ((), ())),
                preferred_element_type=F32,
            ).astype(BF16)
            for i in range(sections)
        ]
    )
    reduced = lax.psum_scatter(in_part, "section", scatter_dimension=0, tiled=True)
    routes = [
        (s * ranks + k, (split * k + s % split) * ranks + s // split)
        for s in range(sections)
        for k in range(ranks)
    ]
    passed_back = lax.ppermute(reduced, ("section", "dp"), routes)[0]

    new_rows = place_rows(place, returned, row_blocks)
    return (passed_back, new_rows)


def solution(mesh):
    in_specs = (
        P("dp", None),
        P("dp", None),
        P("dp", "section"),
        P(None, "dp", "section"),
        P("dp", "section", None),
        P("section", "dp", None, None, None),
        P("section", "dp", None, None, None),
        P("section", "dp", None, None, None),
        P(),
    )
    out_specs = (P("dp", "section"), P(None, "dp", "section"))
    return jax.shard_map(
        per_device, mesh=mesh, in_specs=in_specs, out_specs=out_specs, check_vma=False
    )
```

```python
import jax
import jax.numpy as jnp
from jax import lax
from jax.experimental import pallas as pl
from jax.experimental.pallas import tpu as pltpu
from jax.sharding import PartitionSpec as P

learn_rate = 0.03
beta_one = 0.9
beta_two = 0.95
adam_eps = 1e-08
decay_rate = 0.1

BF16 = jnp.bfloat16
F32 = jnp.float32


CHUNKS = 2
MESH = pl.DeviceIdType.MESH


def spread_kernel(shape, cot_ref, act_ref, cot_out, act_out, held, local_sem, send_sem, recv_sem):
    sections, ranks, tok_dev, cols = shape
    chips = sections // 2
    piece = tok_dev // sections
    s = lax.axis_index("section")
    k = lax.axis_index("dp")
    core = lax.rem(s, 2)
    chip = s // 2
    sibling = (s + 1 - 2 * core, k)
    along = {d: (s, lax.rem(k + d, ranks)) for d in range(1, ranks)}
    across = {j: (2 * lax.rem(chip + j, chips) + core, k) for j in range(1, chips)}

    barrier = pltpu.get_barrier_semaphore()
    greeted = list(along.values()) + list(across.values()) + [sibling]
    for peer in greeted:
        pl.semaphore_signal(barrier, inc=1, device_id=peer, device_id_type=MESH)
    pl.semaphore_wait(barrier, len(greeted))

    pairs = ((cot_ref, cot_out), (act_ref, act_out))
    sems = iter(range(send_sem.shape[0]))

    def send(src, dst, peer):
        at = next(sems)
        copy = pltpu.make_async_remote_copy(
            src_ref=src,
            dst_ref=dst,
            send_sem=send_sem.at[at],
            recv_sem=recv_sem.at[at],
            device_id=peer,
            device_id_type=MESH,
        )
        copy.start()
        return copy

    def rows(out, rank, section):
        start = pl.multiple_of(rank * tok_dev + section * piece, piece)
        return out.at[pl.ds(start, piece), :]

    hops = {}
    for d in range(1, ranks):
        for a, (ref, out) in enumerate(pairs):
            start = pl.multiple_of(along[d][1] * cols, cols)
            from_rows = pl.ds(pl.multiple_of(s * piece, piece), piece)
            hops[a, d] = send(ref.at[from_rows, pl.ds(start, cols)], rows(out, k, s), along[d])
    own_cols = pl.ds(pl.multiple_of(k * cols, cols), cols)
    own_rows = pl.ds(pl.multiple_of(k * tok_dev, tok_dev), tok_dev)
    local = []
    for a, (ref, out) in enumerate(pairs):
        copy = pltpu.make_async_copy(ref.at[:, own_cols], held.at[a], local_sem.at[a])
        copy.start()
        local.append(copy)
    for a, (ref, out) in enumerate(pairs):
        local[a].wait()
        local[a] = pltpu.make_async_copy(held.at[a], out.at[own_rows, :], local_sem.at[2 + a])
        local[a].start()
    wide, last = {}, []
    for d in range(1, ranks):
        origin = lax.rem(k + ranks - d, ranks)
        for a, (ref, out) in enumerate(pairs):
            hops[a, d].wait_recv()
            block = rows(out, origin, s)
            for j in range(1, chips):
                wide[a, d, j] = send(block, block, across[j])
            last.append(send(block, block, sibling))
    for d in range(1, ranks):
        origin = lax.rem(k + ranks - d, ranks)
        for a, (ref, out) in enumerate(pairs):
            for j in range(1, chips):
                wide[a, d, j].wait_recv()
                block = rows(out, origin, 2 * lax.rem(chip + chips - j, chips) + core)
                last.append(send(block, block, sibling))
    for copy in last:
        copy.wait_recv()
    for copy in list(hops.values()) + list(wide.values()) + last:
        copy.wait_send()
    for copy in local:
        copy.wait()


def spread(cotangent, activations, sections, ranks):
    tok_dev, width = activations.shape
    cols = width // ranks
    copies = 2 * (ranks - 1) * sections
    out = jax.ShapeDtypeStruct((ranks * tok_dev, cols), activations.dtype)
    anywhere = pl.BlockSpec(memory_space=pl.ANY)
    moved = 2 * ranks * tok_dev * cols * 2

    def body(*refs):
        spread_kernel((sections, ranks, tok_dev, cols), *refs)

    return pl.pallas_call(
        body,
        out_shape=(out, out),
        in_specs=[anywhere, anywhere],
        out_specs=(anywhere, anywhere),
        scratch_shapes=[
            pltpu.VMEM((2, tok_dev, cols), activations.dtype),
            pltpu.SemaphoreType.DMA((4,)),
            pltpu.SemaphoreType.DMA((copies,)),
            pltpu.SemaphoreType.DMA((copies,)),
        ],
        compiler_params=pltpu.CompilerParams(collective_id=1, has_side_effects=True),
        cost_estimate=pl.CostEstimate(flops=0, bytes_accessed=8 * moved, transcendentals=0),
        name="spread",
    )(cotangent, activations)


def adam_kernel(source_ref, count_ref, fix_ref, grad_ref, w_ref, a_ref, b_ref, out_ref):
    @pl.when(pl.program_id(0) < count_ref[0])
    def _():
        scale_one = learn_rate / fix_ref[0]
        scale_two = 1.0 / fix_ref[1]

        def one(i, carry):
            grad = grad_ref[i].astype(F32)
            first = beta_one * a_ref[i] + (1.0 - beta_one) * grad
            second = beta_two * b_ref[i] + (1.0 - beta_two) * grad * grad
            update = (first * scale_one) / (jnp.sqrt(second * scale_two) + adam_eps)
            out_ref[i] = (w_ref[i] * (1.0 - learn_rate * decay_rate) - update).astype(BF16)
            return carry

        lax.fori_loop(0, grad_ref.shape[0], one, 0)


def adam_slots(sources, count, fixes, arrivals, states, chunk, per_dest):
    total, rows, cols = arrivals.shape
    capacity = states[0].shape[0]
    groups = capacity // per_dest
    cuts = 2

    def at_slot(g, h, source_ref, count_ref):
        live = g < count_ref[0]
        return (
            jnp.minimum(g, jnp.maximum(count_ref[0] - 1, 0)),
            jnp.where(live, h, cuts - 1),
            chunk,
        )

    def at_item(g, h, source_ref, count_ref):
        return (source_ref[g], jnp.where(g < count_ref[0], h, cuts - 1), 0)

    state_spec = pl.BlockSpec((per_dest, rows // cuts, cols), at_slot)
    item_spec = pl.BlockSpec((per_dest, rows // cuts, cols), at_item)
    return pl.pallas_call(
        adam_kernel,
        out_shape=jax.ShapeDtypeStruct(arrivals.shape, BF16),
        grid_spec=pltpu.PrefetchScalarGridSpec(
            num_scalar_prefetch=2,
            grid=(groups, cuts),
            in_specs=[pl.BlockSpec(memory_space=pltpu.SMEM), item_spec] + [state_spec] * 3,
            out_specs=item_spec,
        ),
        cost_estimate=pl.CostEstimate(
            flops=20 * capacity * rows * cols,
            bytes_accessed=16 * capacity * rows * cols,
            transcendentals=capacity * rows * cols,
        ),
        name="adam",
    )(sources, count, fixes, arrivals, *states)


def pick_rows(place, grads, rows, slots):
    cols = grads[0].shape[1]
    count = place.shape[0]
    anywhere = pl.BlockSpec(memory_space=pl.ANY)

    def body(place_ref, up_ref, down_ref, out_ref, sems):
        def copy_of(r, m):
            ref = (up_ref, down_ref)[m]
            start = pl.multiple_of(r * rows, rows)
            return pltpu.make_async_copy(
                ref.at[pl.ds(start, rows), :], out_ref.at[place_ref[2 * r + m]], sems.at[2 * r + m]
            )

        def begin(r, carry):
            copy_of(r, 0).start()
            copy_of(r, 1).start()
            return carry

        def finish(r, carry):
            copy_of(r, 0).wait()
            copy_of(r, 1).wait()
            return carry

        lax.fori_loop(0, count // 2, begin, 0)
        lax.fori_loop(0, count // 2, finish, 0)

    return pl.pallas_call(
        body,
        out_shape=jax.ShapeDtypeStruct((slots, rows, cols), grads[0].dtype),
        in_specs=[
            pl.BlockSpec(memory_space=pltpu.SMEM),
            pl.BlockSpec(memory_space=pltpu.VMEM),
            pl.BlockSpec(memory_space=pltpu.VMEM),
        ],
        out_specs=anywhere,
        scratch_shapes=[pltpu.SemaphoreType.DMA((count,))],
        cost_estimate=pl.CostEstimate(
            flops=0, bytes_accessed=4 * count * rows * cols, transcendentals=0
        ),
        name="pick_rows",
    )(place, *grads)


def place_rows(place, parts, row_blocks):
    rows, cols = parts[0].shape[1:]
    width = cols * len(parts)
    count = row_blocks * 2
    anywhere = pl.BlockSpec(memory_space=pl.ANY)

    def body(place_ref, *refs):
        out_ref, sems = refs[-2:]

        def copies_of(r):
            start = pl.multiple_of(r * rows, rows)
            return [
                pltpu.make_async_copy(
                    ref.at[place_ref[2 * r + m]],
                    out_ref.at[m, pl.ds(start, rows), pl.ds(at * cols, cols)],
                    sems.at[at * count + 2 * r + m],
                )
                for at, ref in enumerate(refs[:-2])
                for m in range(2)
            ]

        def begin(r, carry):
            for copy in copies_of(r):
                copy.start()
            return carry

        def finish(r, carry):
            for copy in copies_of(r):
                copy.wait()
            return carry

        lax.fori_loop(0, row_blocks, begin, 0)
        lax.fori_loop(0, row_blocks, finish, 0)

    return pl.pallas_call(
        body,
        out_shape=jax.ShapeDtypeStruct((2, row_blocks * rows, width), parts[0].dtype),
        in_specs=[pl.BlockSpec(memory_space=pltpu.SMEM)] + [anywhere] * len(parts),
        out_specs=pl.BlockSpec(memory_space=pltpu.VMEM),
        scratch_shapes=[pltpu.SemaphoreType.DMA((count * len(parts),))],
        cost_estimate=pl.CostEstimate(
            flops=0, bytes_accessed=4 * count * rows * width, transcendentals=0
        ),
        name="place_rows",
    )(place, *parts)


def per_device(
    activations, cotangent, gate_pre, weights, holder_map, master, moment_one, moment_two, adam_step
):
    sections = lax.axis_size("section")
    ranks = lax.axis_size("dp")
    here = lax.axis_index("section")
    tok_dev, width = activations.shape
    row_count, hidden_units = weights.shape[1:]
    block_rows = master.shape[3]
    capacity = master.shape[2]
    row_blocks = row_count // block_rows
    per_dest = 4 * row_blocks // sections
    over_tokens = (((0,), (0,)), ((), ()))
    span = hidden_units // CHUNKS if hidden_units % (128 * CHUNKS) == 0 else hidden_units
    chunks = hidden_units // span

    owners = holder_map[:, 0, :].reshape(-1)
    section_ids = jnp.arange(sections, dtype=jnp.int32)
    choose = (owners[:, None] == section_ids[None, :]).astype(jnp.int32)
    totals = jnp.sum(choose, axis=0)
    every_total = lax.all_gather(totals, "section")
    every_total, activations, cotangent = lax.optimization_barrier(
        (every_total, activations, cotangent)
    )
    order_in = jnp.sum((jnp.cumsum(choose, axis=0) - choose) * choose, axis=1)
    place = owners * per_dest + order_in
    mine = jnp.sum(jnp.where(section_ids[None, :] == here, every_total, 0), axis=1)
    live = (mine > 0).astype(jnp.int32)
    rank_of = jnp.cumsum(live) - live
    count = jnp.sum(live)
    groups = jnp.minimum(
        jnp.arange(capacity // per_dest, dtype=jnp.int32), jnp.maximum(count - 1, 0)
    )
    sources = jnp.sum(
        jnp.where(
            (rank_of[None, :] == groups[:, None]) & (live[None, :] > 0), section_ids[None, :], 0
        ),
        axis=1,
    )
    step_float = adam_step[0].astype(F32)
    fixes = jnp.stack(
        [
            1.0 - jnp.power(jnp.float32(beta_one), step_float),
            1.0 - jnp.power(jnp.float32(beta_two), step_float),
        ]
    )
    states = (master[0, 0], moment_one[0, 0], moment_two[0, 0])
    gate_silu = jax.nn.silu(gate_pre.astype(F32))

    cot_full, act_full = spread(cotangent, activations, sections, ranks)

    parts = []
    for j in range(chunks):
        at = slice(j * span, (j + 1) * span)
        parts.append(
            jnp.concatenate(
                [
                    jnp.dot(cot_full, weights[1][:, at], preferred_element_type=F32).astype(BF16),
                    jnp.dot(act_full, weights[0][:, at], preferred_element_type=F32).astype(BF16),
                ],
                axis=1,
            )
        )

    def sum_and_gather(part, gate):
        both = lax.psum_scatter(part, "dp", scatter_dimension=0, tiled=True).astype(F32)
        local = (both * jnp.concatenate([gate, gate], axis=1)).astype(BF16)
        return lax.all_gather(local, "dp", axis=0, tiled=True)

    gates = [gate_silu[:, j * span : (j + 1) * span] for j in range(chunks)]
    gathered, returned = [sum_and_gather(parts[0], gates[0])], []
    up_rows = weights[0]
    for j in range(chunks):
        if j + 1 < chunks:
            gathered[j], parts[j + 1] = lax.optimization_barrier((gathered[j], parts[j + 1]))
        grads = (
            lax.dot_general(
                act_full, gathered[j][:, :span], over_tokens, preferred_element_type=F32
            ).astype(BF16),
            lax.dot_general(
                cot_full, gathered[j][:, span:], over_tokens, preferred_element_type=F32
            ).astype(BF16),
        )
        outgoing = pick_rows(place, grads, block_rows, sections * per_dest)
        if j + 1 < chunks:
            gates[j + 1], outgoing = lax.optimization_barrier((gates[j + 1], outgoing))
            gathered.append(sum_and_gather(parts[j + 1], gates[j + 1]))
        else:
            up_rows, outgoing = lax.optimization_barrier((up_rows, outgoing))
            returned, outgoing = lax.optimization_barrier((returned, outgoing))
        arrivals = lax.all_to_all(outgoing, "section", split_axis=0, concat_axis=0, tiled=True)
        updated = adam_slots(sources, count.reshape(1), fixes, arrivals, states, j, per_dest)
        if j + 1 < chunks:
            act_full, cot_full, updated = lax.optimization_barrier((act_full, cot_full, updated))
        returned.append(
            lax.all_to_all(updated, "section", split_axis=0, concat_axis=0, tiled=True)
        )

    split = sections // ranks
    back_up = jnp.concatenate([each[:, :span] for each in gathered], axis=1)
    up_rows = up_rows.reshape(split, row_count // split, hidden_units)
    in_part = jnp.stack(
        [
            lax.dot_general(
                back_up, up_rows[h], (((1,), (1,)), ((), ())), preferred_element_type=F32
            ).astype(BF16)
            for h in range(split)
        ]
    ).reshape(sections, tok_dev, row_count // split)
    reduced = lax.psum_scatter(in_part, "section", scatter_dimension=0, tiled=True)
    routes = [
        (s * ranks + k, (split * k + s // ranks) * ranks + s % ranks)
        for s in range(sections)
        for k in range(ranks)
    ]
    passed_back = lax.ppermute(reduced, ("section", "dp"), routes)[0]

    new_rows = place_rows(place, returned, row_blocks)
    return (passed_back, new_rows)


def solution(mesh):
    in_specs = (
        P("dp", None),
        P("dp", None),
        P("dp", "section"),
        P(None, "dp", "section"),
        P("dp", "section", None),
        P("section", "dp", None, None, None),
        P("section", "dp", None, None, None),
        P("section", "dp", None, None, None),
        P(),
    )
    out_specs = (P("dp", "section"), P(None, "dp", "section"))
    return jax.shard_map(
        per_device, mesh=mesh, in_specs=in_specs, out_specs=out_specs, check_vma=False
    )
```
